32 devices in a mesh: grp: 4 (over y, core), frm: 8 (over z, x).
Axes of the slice: x: 2, y: 2, z: 4, core: 2. Of those that a mesh axis runs over, the one named last changes fastest.
Arguments:
- latents: bfloat16 [32, 512, 1152], P(('grp', 'frm')), may hold values from -6 to 6
- spatial_weight: bfloat16 [1152, 3456], replicated, may hold values from -1 to 1
- temporal_weight: bfloat16 [1152, 3456], replicated, may hold values from -1 to 1
- out_grad: bfloat16 [32, 512, 1152], P(('grp', 'frm')), may hold values from -6 to 6
Outputs:
- output: bfloat16 [32, 512, 1152], P(('grp', 'frm'))
- in_grad: bfloat16 [32, 512, 1152], P(('grp', 'frm'))
The draws below stay inside these ranges and needn't reach their ends.
All inputs are finite; a program needn't handle non-finite values.
Results may differ from the reference program's by a relative error of at most 0.013.
Values may be sent and summed in bfloat16 or wider, within the bound.
A program may use at most 192 MiB of HBM per device.

```python
import math
import jax
import jax.numpy as jnp
from jax import lax

D = 1152
HEADS = 16
PATCHES = 512
FRAMES = 32


def projection_draw(key, tag):
    keyed = jax.random.fold_in(key, tag)
    parts = jax.random.split(keyed, 1)
    base = jax.random.truncated_normal(parts[0], -3.0, 3.0, (D, 3 * D), jnp.float32) / math.sqrt(D)
    return jnp.clip(base, -1.0, 1.0)


def draw_spatial_weight(key, part):
    return projection_draw(key, 11).astype(jnp.bfloat16)


def draw_temporal_weight(key, part):
    return projection_draw(key, 23).astype(jnp.bfloat16)


def level_of(key, extent, cuts, least, top_value):
    loudness, own = 1.0, jax.random.fold_in(key, 6)
    for position, blocks in cuts:
        heights = jnp.exp(jax.random.uniform(jax.random.fold_in(own, position), (blocks,), jnp.float32, least / len(cuts), top_value / len(cuts)))
        loudness = loudness * jnp.repeat(heights, extent[position] // blocks).reshape([-1 if axis == position else 1 for axis in range(len(extent))])
    return loudness


def scatter_about(key, dims, scale, limit, cuts=(), held_as=jnp.bfloat16):
    values = jax.random.normal(key, dims, jnp.float32) * scale
    if len(cuts) > 0:
        values = level_of(key, dims, cuts, -0.22, 0.18) * values
    return jnp.clip(values, min=-limit, max=limit).astype(held_as)


def setup_inputs(seed: int = 0) -> dict:
    key_list = jax.random.split(jax.random.key(seed), 5)
    return {
        "latents": scatter_about(key_list[0], (FRAMES, PATCHES, D), 1.0, 6.0, ((0, 32),)),
        "spatial_weight": draw_spatial_weight(jax.random.fold_in(key_list[4], 71), 0),
        "temporal_weight": draw_temporal_weight(jax.random.fold_in(key_list[4], 71), 0),
        "out_grad": scatter_about(key_list[3], (FRAMES, PATCHES, D), 1.0, 6.0, ((0, 32),)),
    }


def normed(tokens):
    values = tokens.astype(jnp.float32)
    center = values - lax.optimization_barrier(jnp.mean(values, axis=-1, keepdims=True))
    spread = lax.optimization_barrier(jnp.mean(center * center, axis=-1, keepdims=True))
    return (center * lax.rsqrt(spread + 1e-06)).astype(jnp.bfloat16)

def attend_block(tokens, weight, over_first):
    first, second, width = tokens.shape
    head_dim = width // HEADS
    rows = normed(tokens).reshape(first * second, width)
    mixed = jnp.dot(rows, weight, preferred_element_type=jnp.float32).astype(jnp.bfloat16)
    mixed = mixed.reshape(first, second, 3, HEADS, head_dim).astype(jnp.float32)
    query, keys, values = (mixed[:, :, 0], mixed[:, :, 1], mixed[:, :, 2])
    if over_first:
        scores = jnp.einsum('pshe,tshe->shpt', query, keys)
    else:
        scores = jnp.einsum('sphe,sqhe->shpq', query, keys)
    scores = scores * (1.0 / math.sqrt(head_dim))
    top = lax.optimization_barrier(jnp.max(scores, axis=-1, keepdims=True))
    expd = jnp.exp(scores - top)
    probs = (expd / lax.optimization_barrier(jnp.sum(expd, axis=-1, keepdims=True))).astype(jnp.bfloat16).astype(jnp.float32)
    if over_first:
        mixout = jnp.einsum('shpt,tshe->pshe', probs, values)
    else:
        mixout = jnp.einsum('shpq,sqhe->sphe', probs, values)
    return (tokens.astype(jnp.float32) + mixout.reshape(first, second, width)).astype(jnp.bfloat16)

def spatial_frame(frame, weight):
    return attend_block(frame[None], weight, False)[0]

def temporal_group(group, weight):
    return attend_block(group, weight, True)

def forward(latents, spatial_weight, temporal_weight):
    frames, patches, width = latents.shape
    spatial_fn = jax.checkpoint(spatial_frame)
    temporal_fn = jax.checkpoint(temporal_group)
    hidden = lax.map(lambda frame: spatial_fn(frame, spatial_weight), latents)
    block_size = min(patches, 16)
    grouped = hidden.reshape(frames, patches // block_size, block_size, width).transpose(1, 0, 2, 3)
    result = lax.map(lambda group: temporal_fn(group, temporal_weight), grouped)
    return result.transpose(1, 0, 2, 3).reshape(frames, patches, width)

def reference(latents, spatial_weight, temporal_weight, out_grad):
    output, pullback = jax.vjp(lambda tokens: forward(tokens, spatial_weight, temporal_weight), latents)
    in_grad = pullback(out_grad)[0]
    return (output, in_grad)
```

```python
import functools
import math

import jax
import jax.numpy as jnp
from jax import lax
from jax.experimental import pallas as pl
from jax.experimental.pallas import tpu as pltpu
from jax.sharding import PartitionSpec as P

HEADS = 16
LANES = 128
WIN = 256
TILE = 384
F32 = jnp.float32
BF16 = jnp.bfloat16
LOG2E = math.log2(math.e)
VMEM_LIMIT = 60 * 1024 * 1024


def mm(a, b):
    return jnp.dot(a, b, preferred_element_type=F32)


def mm_bt(a, b):
    return lax.dot_general(a, b, (((1,), (1,)), ((), ())), preferred_element_type=F32)


def mm_at(a, b):
    return lax.dot_general(a, b, (((0,), (0,)), ((), ())), preferred_element_type=F32)


def window(head, head_dim, width):
    first = head * head_dim
    start = jnp.minimum(first // LANES, (width - WIN) // LANES) * LANES
    lane = lax.broadcasted_iota(jnp.int32, (1, WIN), 1) + start
    own = ((lane >= first) & (lane < first + head_dim)).astype(F32)
    return pl.multiple_of(start, LANES), own


def center_scale(tokens):
    values = tokens.astype(F32)
    center = values - jnp.mean(values, axis=-1, keepdims=True)
    spread = jnp.mean(center * center, axis=-1, keepdims=True)
    return center, lax.rsqrt(spread + 1e-06)


def norm_pull(tokens, cot):
    center, scale = center_scale(tokens)
    unit = center * scale
    return scale * (
        cot - jnp.mean(cot, axis=-1, keepdims=True) - unit * jnp.mean(cot * unit, axis=-1, keepdims=True)
    )


def project(rows_ref, weight_ref, mixed_ref):
    @pl.loop(0, weight_ref.shape[1] // TILE)
    def _(step):
        columns = pl.ds(pl.multiple_of(step * TILE, LANES), TILE)
        mixed_ref[:, columns] = mm(rows_ref[...], weight_ref[:, columns]).astype(BF16)


def project_pull(cots_ref, weight_ref, grad_ref):
    @pl.loop(0, weight_ref.shape[0] // TILE)
    def _(step):
        columns = pl.ds(pl.multiple_of(step * TILE, LANES), TILE)
        grad_ref[:, columns] = mm_bt(cots_ref[...], weight_ref[columns, :])


def spatial_kernel(x_ref, w_ref, hidden_ref, mixed_ref, expd_ref, out_ref, inv_ref, rows_ref):
    head = pl.program_id(0)
    tokens, width = x_ref.shape
    head_dim = width // HEADS
    rate = LOG2E / math.sqrt(head_dim)

    @pl.when(head == 0)
    def _():
        center, scale = center_scale(x_ref[...])
        rows_ref[...] = (center * scale).astype(BF16)
        project(rows_ref, w_ref, mixed_ref)
        out_ref[...] = jnp.zeros_like(out_ref)
        inv_ref[...] = jnp.zeros_like(inv_ref)

    start, own = window(head, head_dim, width)
    ownb = own.astype(BF16)
    cols = pl.ds(start, WIN)
    keys = mixed_ref[:, pl.ds(start + width, WIN)]
    values = mixed_ref[:, pl.ds(start + 2 * width, WIN)] * ownb + (1 - own).astype(BF16)
    block = tokens // 2
    for part in range(2):
        rows = slice(part * block, (part + 1) * block)
        query = mixed_ref[rows, cols] * ownb
        scores = mm_bt(query, keys)
        top = jnp.max(scores, axis=-1, keepdims=True)
        expd = jnp.exp2((scores - top) * rate).astype(BF16)
        expd_ref[0, rows, :] = expd
        mixout = mm(expd, values)
        total = jnp.max(mixout * (1 - own), axis=-1, keepdims=True)
        inv = own / total
        out_ref[rows, cols] += mixout * inv
        inv_ref[rows, cols] += inv

    @pl.when(head == HEADS - 1)
    def _():
        hidden_ref[...] = (x_ref[...].astype(F32) + out_ref[...]).astype(BF16)


def spatial_forward(x, w):
    tokens, width = x.shape
    full = lambda shape: pl.BlockSpec(shape, lambda h: (0, 0), pipeline_mode=pl.Buffered(1))
    return pl.pallas_call(
        spatial_kernel,
        grid=(HEADS,),
        in_specs=[full(x.shape), full(w.shape)],
        out_specs=[
            full(x.shape),
            full((tokens, 3 * width)),
            pl.BlockSpec((1, tokens, tokens), lambda h: (h, 0, 0)),
            full(x.shape),
            full(x.shape),
        ],
        out_shape=[
            jax.ShapeDtypeStruct(x.shape, BF16),
            jax.ShapeDtypeStruct((tokens, 3 * width), BF16),
            jax.ShapeDtypeStruct((HEADS, tokens, tokens), BF16),
            jax.ShapeDtypeStruct(x.shape, F32),
            jax.ShapeDtypeStruct(x.shape, F32),
        ],
        scratch_shapes=[pltpu.VMEM(x.shape, BF16)],
        compiler_params=pltpu.CompilerParams(vmem_limit_bytes=VMEM_LIMIT),
        cost_estimate=pl.CostEstimate(flops=8 * 10**9, bytes_accessed=30 * 10**6, transcendentals=4 * 10**6),
        name="spatial_fwd",
    )(x, w)


def spatial_pull_kernel(g_ref, x_ref, mixed_ref, out_ref, inv_ref, expd_ref, w_ref, grad_ref, acc_ref, cots_ref, rows_ref):
    head = pl.program_id(0)
    tokens, width = x_ref.shape
    head_dim = width // HEADS

    @pl.when(head == 0)
    def _():
        acc_ref[...] = jnp.zeros_like(acc_ref)

    start, own = window(head, head_dim, width)
    ownb = own.astype(BF16)
    cols = pl.ds(start, WIN)
    kcols = pl.ds(start + width, WIN)
    vcols = pl.ds(start + 2 * width, WIN)
    keys = mixed_ref[:, kcols]
    values = mixed_ref[:, vcols]
    block = tokens // 2
    dkeys = dvalues = None
    for part in range(2):
        rows = slice(part * block, (part + 1) * block)
        dmix = g_ref[rows, cols].astype(F32) * (inv_ref[rows, cols] * own)
        delta = jnp.sum(dmix * out_ref[rows, cols], axis=-1, keepdims=True)
        dmix = dmix.astype(BF16)
        expd = expd_ref[0, rows, :]
        dprobs = mm_bt(dmix, values)
        dscores = (expd.astype(F32) * (dprobs - delta)).astype(BF16)
        acc_ref[rows, cols] += mm(dscores, keys * ownb)
        dk = mm_at(dscores, mixed_ref[rows, cols] * ownb)
        dv = mm_at(expd, dmix)
        dkeys = dk if dkeys is None else dkeys + dk
        dvalues = dv if dvalues is None else dvalues + dv
    acc_ref[:, kcols] += dkeys
    acc_ref[:, vcols] += dvalues

    @pl.when(head == HEADS - 1)
    def _():
        scale = 1.0 / math.sqrt(head_dim)
        cots_ref[:, : 2 * width] = (acc_ref[:, : 2 * width] * scale).astype(BF16)
        cots_ref[:, 2 * width :] = acc_ref[:, 2 * width :].astype(BF16)
        project_pull(cots_ref, w_ref, rows_ref)
        grad_ref[...] = (g_ref[...].astype(F32) + norm_pull(x_ref[...], rows_ref[...])).astype(BF16)


def spatial_pull(g, x, mixed, out, inv, expd, w):
    tokens, width = x.shape
    full = lambda a: pl.BlockSpec(a.shape, lambda h: (0, 0), pipeline_mode=pl.Buffered(1))
    return pl.pallas_call(
        spatial_pull_kernel,
        grid=(HEADS,),
        in_specs=[full(g), full(x), full(mixed), full(out), full(inv),
                  pl.BlockSpec((1, tokens, tokens), lambda h: (h, 0, 0)), full(w)],
        out_specs=full(x),
        out_shape=jax.ShapeDtypeStruct(x.shape, BF16),
        scratch_shapes=[
            pltpu.VMEM((tokens, 3 * width), F32),
            pltpu.VMEM((tokens, 3 * width), BF16),
            pltpu.VMEM((tokens, width), F32),
        ],
        compiler_params=pltpu.CompilerParams(vmem_limit_bytes=VMEM_LIMIT),
        cost_estimate=pl.CostEstimate(flops=12 * 10**9, bytes_accessed=30 * 10**6, transcendentals=10**4),
        name="spatial_bwd",
    )(g, x, mixed, out, inv, expd, w)


def reorder(rows, inner, outer):
    row = lax.broadcasted_iota(jnp.int32, (rows, rows), 0)
    column = lax.broadcasted_iota(jnp.int32, (rows, rows), 1)
    return (column == (row % outer) * inner + row // outer).astype(F32).astype(BF16)


def temporal_kernel(frames, z_ref, g_ref, w_ref, res_ref, grad_ref, zt_ref, gt_ref, rows_ref, mixed_ref, out_ref, acc_ref, cots_ref):
    tokens, width = z_ref.shape
    head_dim = width // HEADS
    rate = LOG2E / math.sqrt(head_dim)
    patches = tokens // frames
    group = max(LANES, frames)

    order = reorder(tokens, patches, frames)
    zt_ref[...] = mm(order, z_ref[...]).astype(BF16)
    gt_ref[...] = mm(order, g_ref[...]).astype(BF16)
    center, scale = center_scale(zt_ref[...])
    rows_ref[...] = (center * scale).astype(BF16)
    project(rows_ref, w_ref, mixed_ref)
    out_ref[...] = jnp.zeros_like(out_ref)
    acc_ref[...] = jnp.zeros_like(acc_ref)
    same = (
        lax.broadcasted_iota(jnp.int32, (group, group), 0) // frames
        == lax.broadcasted_iota(jnp.int32, (group, group), 1) // frames
    )

    @pl.loop(0, HEADS)
    def _(head):
        start, own = window(head, head_dim, width)
        ownb = own.astype(BF16)
        cols = pl.ds(start, WIN)
        kcols = pl.ds(pl.multiple_of(start + width, LANES), WIN)
        vcols = pl.ds(pl.multiple_of(start + 2 * width, LANES), WIN)
        spans = [slice(part * group, (part + 1) * group) for part in range(tokens // group)]
        query = [mixed_ref[rows, cols] * ownb for rows in spans]
        keys = [mixed_ref[rows, kcols] * ownb for rows in spans]
        values = [mixed_ref[rows, vcols] * ownb for rows in spans]
        grads = [gt_ref[rows, cols].astype(F32) for rows in spans]
        scores = [jnp.where(same, mm_bt(q, k), -3e38) for q, k in zip(query, keys)]
        expd = [
            jnp.exp2((s - jnp.max(s, axis=-1, keepdims=True)) * rate).astype(BF16) for s in scores
        ]
        ones = (1 - own).astype(BF16)
        mixout = [mm(e, v + ones) for e, v in zip(expd, values)]
        inv = [own / jnp.max(m * (1 - own), axis=-1, keepdims=True) for m in mixout]
        mixout = [m * i for m, i in zip(mixout, inv)]
        dmix = [g * i for g, i in zip(grads, inv)]
        delta = [jnp.sum(d * m, axis=-1, keepdims=True) for d, m in zip(dmix, mixout)]
        dmix = [d.astype(BF16) for d in dmix]
        dscores = [
            (e.astype(F32) * (mm_bt(d, v) - t)).astype(BF16)
            for e, d, v, t in zip(expd, dmix, values, delta)
        ]
        dquery = [mm(s, k) for s, k in zip(dscores, keys)]
        dkeys = [mm_at(s, q) for s, q in zip(dscores, query)]
        dvalues = [mm_at(e, d) for e, d in zip(expd, dmix)]
        for rows, m, dq, dk, dv in zip(spans, mixout, dquery, dkeys, dvalues):
            out_ref[rows, cols] += m
            acc_ref[rows, cols] += dq
            acc_ref[rows, kcols] += dk
            acc_ref[rows, vcols] += dv

    scale = 1.0 / math.sqrt(head_dim)
    cots_ref[:, : 2 * width] = (acc_ref[:, : 2 * width] * scale).astype(BF16)
    cots_ref[:, 2 * width :] = acc_ref[:, 2 * width :].astype(BF16)
    rows_ref[...] = (zt_ref[...].astype(F32) + out_ref[...]).astype(BF16)
    project_pull(cots_ref, w_ref, out_ref)
    zt_ref[...] = (gt_ref[...].astype(F32) + norm_pull(zt_ref[...], out_ref[...])).astype(BF16)
    order = reorder(tokens, frames, patches)
    grad_ref[...] = mm(order, zt_ref[...]).astype(BF16)
    res_ref[...] = mm(order, rows_ref[...]).astype(BF16)


def temporal_both(z, g, w, frames):
    tokens, width = z.shape
    return pl.pallas_call(
        functools.partial(temporal_kernel, frames),
        out_shape=[jax.ShapeDtypeStruct(z.shape, BF16)] * 2,
        in_specs=[pl.BlockSpec(memory_space=pltpu.VMEM)] * 3,
        out_specs=[pl.BlockSpec(memory_space=pltpu.VMEM)] * 2,
        scratch_shapes=[
            pltpu.VMEM(z.shape, BF16),
            pltpu.VMEM(z.shape, BF16),
            pltpu.VMEM(z.shape, BF16),
            pltpu.VMEM((tokens, 3 * width), BF16),
            pltpu.VMEM(z.shape, F32),
            pltpu.VMEM((tokens, 3 * width), F32),
            pltpu.VMEM((tokens, 3 * width), BF16),
        ],
        compiler_params=pltpu.CompilerParams(vmem_limit_bytes=VMEM_LIMIT),
        cost_estimate=pl.CostEstimate(flops=12 * 10**9, bytes_accessed=15 * 10**6, transcendentals=10**6),
        name="temporal",
    )(z, g, w)


def swap(items):
    return lax.all_to_all(items, ("grp", "frm"), split_axis=0, concat_axis=0, tiled=True)


def local(frames, latents, spatial_weight, temporal_weight, out_grad):
    x = latents[0]
    grad_cols = swap(out_grad[0])
    hidden, mixed, expd, out, inv = spatial_forward(x, spatial_weight)
    hidden_cols = swap(hidden)
    result_cols, hidden_grad_cols = temporal_both(hidden_cols, grad_cols, temporal_weight, frames)
    hidden_grad = swap(hidden_grad_cols)
    output = swap(result_cols)
    in_grad = spatial_pull(hidden_grad, x, mixed, out, inv, expd, spatial_weight)
    return (output[None], in_grad[None])


def solution(mesh):
    frames = mesh.shape["grp"] * mesh.shape["frm"]
    return jax.shard_map(
        functools.partial(local, frames),
        mesh=mesh,
        in_specs=(P(("grp", "frm"), None, None), P(), P(), P(("grp", "frm"), None, None)),
        out_specs=(P(("grp", "frm"), None, None), P(("grp", "frm"), None, None)),
        check_vma=False,
    )
```

```python
import functools
import math

import jax
import jax.numpy as jnp
from jax import lax
from jax.experimental import pallas as pl
from jax.experimental.pallas import tpu as pltpu
from jax.sharding import PartitionSpec as P


HEADS = 16
LANES = 128
WIN = 256
TILE = 384
CHUNKS = 2
CHAINS = 8
F32 = jnp.float32
BF16 = jnp.bfloat16
LOG2E = math.log2(math.e)
VMEM_LIMIT = 60 * 1024 * 1024


def mm(a, b):
    return jnp.dot(a, b, preferred_element_type=F32)


def mm_bt(a, b):
    return lax.dot_general(a, b, (((1,), (1,)), ((), ())), preferred_element_type=F32)


def mm_at(a, b):
    return lax.dot_general(a, b, (((0,), (0,)), ((), ())), preferred_element_type=F32)


def window(head, head_dim, width):
    first = head * head_dim
    start = jnp.minimum(first // LANES, (width - WIN) // LANES) * LANES
    lane = lax.broadcasted_iota(jnp.int32, (1, WIN), 1) + start
    own = ((lane >= first) & (lane < first + head_dim)).astype(F32)
    return pl.multiple_of(start, LANES), own


def center_scale(tokens):
    values = tokens.astype(F32)
    center = values - jnp.mean(values, axis=-1, keepdims=True)
    spread = jnp.mean(center * center, axis=-1, keepdims=True)
    return center, lax.rsqrt(spread + 1e-06)


def norm_pull(tokens, cot):
    center, scale = center_scale(tokens)
    unit = center * scale
    return scale * (
        cot - jnp.mean(cot, axis=-1, keepdims=True) - unit * jnp.mean(cot * unit, axis=-1, keepdims=True)
    )


def project(rows_ref, weight_ref, mixed_ref):
    @pl.loop(0, weight_ref.shape[1] // TILE)
    def _(step):
        columns = pl.ds(pl.multiple_of(step * TILE, LANES), TILE)
        mixed_ref[:, columns] = mm(rows_ref[...], weight_ref[:, columns]).astype(BF16)


def project_pull(cots_ref, weight_ref, grad_ref):
    @pl.loop(0, weight_ref.shape[0] // TILE)
    def _(step):
        columns = pl.ds(pl.multiple_of(step * TILE, LANES), TILE)
        grad_ref[:, columns] = mm_bt(cots_ref[...], weight_ref[columns, :])


def spatial_kernel(x_ref, w_ref, *refs):
    hidden_refs, (mixed_ref, expd_ref, out_ref, inv_ref, rows_ref) = refs[:CHUNKS], refs[CHUNKS:]
    head = pl.program_id(0)
    tokens, width = x_ref.shape
    head_dim = width // HEADS
    rate = LOG2E / math.sqrt(head_dim)

    @pl.when(head == 0)
    def _():
        center, scale = center_scale(x_ref[...])
        rows_ref[...] = (center * scale).astype(BF16)
        project(rows_ref, w_ref, mixed_ref)
        out_ref[...] = jnp.zeros_like(out_ref)
        inv_ref[...] = jnp.zeros_like(inv_ref)

    start, own = window(head, head_dim, width)
    ownb = own.astype(BF16)
    cols = pl.ds(start, WIN)
    keys = mixed_ref[:, pl.ds(start + width, WIN)]
    values = mixed_ref[:, pl.ds(start + 2 * width, WIN)] * ownb + (1 - own).astype(BF16)
    block = tokens // CHUNKS
    half = tokens // 2
    spans = [slice(0, half), slice(half, tokens)]
    scores = [mm_bt(mixed_ref[rows, cols] * ownb, keys) for rows in spans]
    expd = [jnp.exp2((s - jnp.max(s, axis=-1, keepdims=True)) * rate).astype(BF16) for s in scores]
    mixout = [mm(e, values) for e in expd]
    inv = [own / jnp.max(m * (1 - own), axis=-1, keepdims=True) for m in mixout]
    for rows, e, m, i in zip(spans, expd, mixout, inv):
        expd_ref[0, rows, :] = e
        out_ref[rows, cols] += m * i
        inv_ref[rows, cols] += i

    @pl.when(head == HEADS - 1)
    def _():
        for part, hidden_ref in enumerate(hidden_refs):
            rows = slice(part * block, (part + 1) * block)
            hidden_ref[...] = (x_ref[rows, :].astype(F32) + out_ref[rows, :]).astype(BF16)


def spatial_forward(x, w):
    tokens, width = x.shape
    full = lambda shape: pl.BlockSpec(shape, lambda h: (0, 0), pipeline_mode=pl.Buffered(1))
    return pl.pallas_call(
        spatial_kernel,
        grid=(HEADS,),
        in_specs=[full(x.shape), full(w.shape)],
        out_specs=[full((tokens // CHUNKS, width))] * CHUNKS + [
            full((tokens, 3 * width)),
            pl.BlockSpec((1, tokens, tokens), lambda h: (h, 0, 0)),
            full(x.shape),
            full(x.shape),
        ],
        out_shape=[jax.ShapeDtypeStruct((tokens // CHUNKS, width), BF16)] * CHUNKS + [
            jax.ShapeDtypeStruct((tokens, 3 * width), BF16),
            jax.ShapeDtypeStruct((HEADS, tokens, tokens), BF16),
            jax.ShapeDtypeStruct(x.shape, F32),
            jax.ShapeDtypeStruct(x.shape, F32),
        ],
        scratch_shapes=[pltpu.VMEM(x.shape, BF16)],
        compiler_params=pltpu.CompilerParams(vmem_limit_bytes=VMEM_LIMIT),
        cost_estimate=pl.CostEstimate(flops=8 * 10**9, bytes_accessed=30 * 10**6, transcendentals=4 * 10**6),
        name="spatial_fwd",
    )(x, w)


def spatial_pull_kernel(*refs):
    g_refs = refs[:CHUNKS]
    (x_ref, mixed_ref, out_ref, inv_ref, expd_ref, w_ref, grad_ref, acc_ref, cots_ref, rows_ref) = refs[CHUNKS:]
    head = pl.program_id(0)
    tokens, width = x_ref.shape
    head_dim = width // HEADS

    @pl.when(head == 0)
    def _():
        acc_ref[...] = jnp.zeros_like(acc_ref)

    start, own = window(head, head_dim, width)
    ownb = own.astype(BF16)
    cols = pl.ds(start, WIN)
    kcols = pl.ds(start + width, WIN)
    vcols = pl.ds(start + 2 * width, WIN)
    keys = mixed_ref[:, kcols]
    values = mixed_ref[:, vcols]
    block = tokens // CHUNKS
    dkeys = dvalues = None
    for part in range(CHUNKS):
        rows = slice(part * block, (part + 1) * block)
        dmix = g_refs[part][:, cols].astype(F32) * (inv_ref[rows, cols] * own)
        delta = jnp.sum(dmix * out_ref[rows, cols], axis=-1, keepdims=True)
        dmix = dmix.astype(BF16)
        expd = expd_ref[0, rows, :]
        dprobs = mm_bt(dmix, values)
        dscores = (expd.astype(F32) * (dprobs - delta)).astype(BF16)
        acc_ref[rows, cols] += mm(dscores, keys * ownb)
        dk = mm_at(dscores, mixed_ref[rows, cols] * ownb)
        dv = mm_at(expd, dmix)
        dkeys = dk if dkeys is None else dkeys + dk
        dvalues = dv if dvalues is None else dvalues + dv
    acc_ref[:, kcols] += dkeys
    acc_ref[:, vcols] += dvalues

    @pl.when(head == HEADS - 1)
    def _():
        scale = 1.0 / math.sqrt(head_dim)
        cots_ref[:, : 2 * width] = (acc_ref[:, : 2 * width] * scale).astype(BF16)
        cots_ref[:, 2 * width :] = acc_ref[:, 2 * width :].astype(BF16)
        project_pull(cots_ref, w_ref, rows_ref)
        for part, g_ref in enumerate(g_refs):
            rows = slice(part * block, (part + 1) * block)
            pulled = norm_pull(x_ref[rows, :], rows_ref[rows, :])
            grad_ref[rows, :] = (g_ref[...].astype(F32) + pulled).astype(BF16)


def spatial_pull(grads, x, mixed, out, inv, expd, w):
    tokens, width = x.shape
    full = lambda a: pl.BlockSpec(a.shape, lambda h: (0, 0), pipeline_mode=pl.Buffered(1))
    return pl.pallas_call(
        spatial_pull_kernel,
        grid=(HEADS,),
        in_specs=[full(g) for g in grads] + [full(x), full(mixed), full(out), full(inv),
                  pl.BlockSpec((1, tokens, tokens), lambda h: (h, 0, 0)), full(w)],
        out_specs=full(x),
        out_shape=jax.ShapeDtypeStruct(x.shape, BF16),
        scratch_shapes=[
            pltpu.VMEM((tokens, 3 * width), F32),
            pltpu.VMEM((tokens, 3 * width), BF16),
            pltpu.VMEM((tokens, width), F32),
        ],
        compiler_params=pltpu.CompilerParams(vmem_limit_bytes=VMEM_LIMIT),
        cost_estimate=pl.CostEstimate(flops=12 * 10**9, bytes_accessed=30 * 10**6, transcendentals=10**4),
        name="spatial_bwd",
    )(*grads, x, mixed, out, inv, expd, w)


def reorder(rows, inner, outer):
    row = lax.broadcasted_iota(jnp.int32, (rows, rows), 0)
    column = lax.broadcasted_iota(jnp.int32, (rows, rows), 1)
    return (column == (row % outer) * inner + row // outer).astype(F32).astype(BF16)


def temporal_kernel(frames, z_ref, g_ref, w_ref, res_ref, grad_ref, zt_ref, gt_ref, rows_ref, mixed_ref, out_ref, acc_ref, cots_ref):
    tokens, width = z_ref.shape
    head_dim = width // HEADS
    rate = LOG2E / math.sqrt(head_dim)
    patches = tokens // frames
    group = max(LANES, frames)

    order = reorder(tokens, patches, frames)
    zt_ref[...] = mm(order, z_ref[...]).astype(BF16)
    gt_ref[...] = mm(order, g_ref[...]).astype(BF16)
    center, scale = center_scale(zt_ref[...])
    rows_ref[...] = (center * scale).astype(BF16)
    project(rows_ref, w_ref, mixed_ref)
    out_ref[...] = jnp.zeros_like(out_ref)
    acc_ref[...] = jnp.zeros_like(acc_ref)
    same = (
        lax.broadcasted_iota(jnp.int32, (group, group), 0) // frames
        == lax.broadcasted_iota(jnp.int32, (group, group), 1) // frames
    )

    spans = [slice(part * group, (part + 1) * group) for part in range(tokens // group)]
    batch = min(HEADS, max(1, CHAINS // len(spans)))

    @pl.loop(0, HEADS // batch)
    def _(step):
        sites = []
        for offset in range(batch):
            start, own = window(step * batch + offset, head_dim, width)
            cols = pl.ds(start, WIN)
            kcols = pl.ds(pl.multiple_of(start + width, LANES), WIN)
            vcols = pl.ds(pl.multiple_of(start + 2 * width, LANES), WIN)
            sites += [(rows, cols, kcols, vcols, own) for rows in spans]
        owns = [site[4] for site in sites]
        query = [mixed_ref[r, c] * o.astype(BF16) for r, c, _, _, o in sites]
        keys = [mixed_ref[r, c] * o.astype(BF16) for r, _, c, _, o in sites]
        values = [mixed_ref[r, c] * o.astype(BF16) for r, _, _, c, o in sites]
        grads = [gt_ref[r, c].astype(F32) for r, c, _, _, _ in sites]
        scores = [jnp.where(same, mm_bt(q, k), -3e38) for q, k in zip(query, keys)]
        expd = [
            jnp.exp2((s - jnp.max(s, axis=-1, keepdims=True)) * rate).astype(BF16) for s in scores
        ]
        mixout = [mm(e, v + (1 - o).astype(BF16)) for e, v, o in zip(expd, values, owns)]
        inv = [o / jnp.max(m * (1 - o), axis=-1, keepdims=True) for m, o in zip(mixout, owns)]
        mixout = [m * i for m, i in zip(mixout, inv)]
        dmix = [g * i for g, i in zip(grads, inv)]
        delta = [jnp.sum(d * m, axis=-1, keepdims=True) for d, m in zip(dmix, mixout)]
        dmix = [d.astype(BF16) for d in dmix]
        dscores = [
            (e.astype(F32) * (mm_bt(d, v) - t)).astype(BF16)
            for e, d, v, t in zip(expd, dmix, values, delta)
        ]
        dquery = [mm(s, k) for s, k in zip(dscores, keys)]
        dkeys = [mm_at(s, q) for s, q in zip(dscores, query)]
        dvalues = [mm_at(e, d) for e, d in zip(expd, dmix)]
        for (r, c, kc, vc, _), m, dq, dk, dv in zip(sites, mixout, dquery, dkeys, dvalues):
            out_ref[r, c] += m
            acc_ref[r, c] += dq
            acc_ref[r, kc] += dk
            acc_ref[r, vc] += dv

    scale = 1.0 / math.sqrt(head_dim)
    cots_ref[:, : 2 * width] = (acc_ref[:, : 2 * width] * scale).astype(BF16)
    cots_ref[:, 2 * width :] = acc_ref[:, 2 * width :].astype(BF16)
    rows_ref[...] = (zt_ref[...].astype(F32) + out_ref[...]).astype(BF16)
    project_pull(cots_ref, w_ref, out_ref)
    zt_ref[...] = (gt_ref[...].astype(F32) + norm_pull(zt_ref[...], out_ref[...])).astype(BF16)
    order = reorder(tokens, frames, patches)
    grad_ref[...] = mm(order, zt_ref[...]).astype(BF16)
    res_ref[...] = mm(order, rows_ref[...]).astype(BF16)


def temporal_both(z, g, w, frames):
    tokens, width = z.shape
    return pl.pallas_call(
        functools.partial(temporal_kernel, frames),
        out_shape=[jax.ShapeDtypeStruct(z.shape, BF16)] * 2,
        in_specs=[pl.BlockSpec(memory_space=pltpu.VMEM)] * 3,
        out_specs=[pl.BlockSpec(memory_space=pltpu.VMEM)] * 2,
        scratch_shapes=[
            pltpu.VMEM(z.shape, BF16),
            pltpu.VMEM(z.shape, BF16),
            pltpu.VMEM(z.shape, BF16),
            pltpu.VMEM((tokens, 3 * width), BF16),
            pltpu.VMEM(z.shape, F32),
            pltpu.VMEM((tokens, 3 * width), F32),
            pltpu.VMEM((tokens, 3 * width), BF16),
        ],
        compiler_params=pltpu.CompilerParams(vmem_limit_bytes=VMEM_LIMIT),
        cost_estimate=pl.CostEstimate(flops=12 * 10**9, bytes_accessed=15 * 10**6, transcendentals=10**6),
        name="temporal",
    )(z, g, w)


def swap(items, axis=0):
    return lax.all_to_all(items, ("grp", "frm"), split_axis=axis, concat_axis=axis, tiled=True)


def local(frames, latents, spatial_weight, temporal_weight, out_grad):
    x, grad = latents[0], out_grad[0]
    tokens, width = x.shape
    shape = (CHUNKS, frames, tokens // (CHUNKS * frames), width)
    grad_cols = swap(grad.reshape(shape), 1)
    grad_cols = grad_cols.reshape(CHUNKS, tokens // CHUNKS, width)
    *hidden, mixed, expd, out, inv = spatial_forward(x, spatial_weight)
    hidden_cols = [swap(piece) for piece in hidden]
    results, hidden_grads = [], []
    for part, piece in enumerate(hidden_cols):
        result, pulled = temporal_both(piece, grad_cols[part], temporal_weight, frames)
        results.append(result)
        hidden_grads.append(swap(pulled))
    results, hidden_grads = lax.optimization_barrier((results, hidden_grads))
    stacked = jnp.stack(results).reshape(shape)
    output = swap(stacked, 1)
    output = output.reshape(tokens, width)
    in_grad = spatial_pull(hidden_grads, x, mixed, out, inv, expd, spatial_weight)
    return (output[None], in_grad[None])


def solution(mesh):
    frames = mesh.shape["grp"] * mesh.shape["frm"]

    def body(*args):
        return local(frames, *args)

    return jax.shard_map(
        body,
        mesh=mesh,
        in_specs=(P(("grp", "frm"), None, None), P(), P(), P(("grp", "frm"), None, None)),
        out_specs=(P(("grp", "frm"), None, None), P(("grp", "frm"), None, None)),
        check_vma=False,
    )
```
